512 devices in a mesh: bead: 32 (over z, x_hi, core), space: 16 (over y, x_lo).
Axes of the slice: x: 4 (x_hi: 2, x_lo: 2; x = x_hi * 2 + x_lo), y: 8, z: 8, core: 2. Of those that a mesh axis runs over, the one named last changes fastest.
Arguments:
- positions: float32 [3, 32, 65536], P(None, 'bead', 'space'), may hold values from -0.12 to 2.12
- momenta: float32 [3, 32, 65536], P(None, 'bead', 'space'), may hold values from -6 to 6
- atom_types: int32 [65536], P('space'), may hold values from 0 to 3
- neighbours: int32 [512, 5], P('space'), may hold values from 0 to 511, as said below
- thermal_noise: float32 [2, 3, 32, 65536], P(None, None, 'bead', 'space'), may hold values from -6 to 6
Outputs:
- positions_out: float32 [3, 32, 65536], P(None, 'bead', 'space')
- momenta_out: float32 [3, 32, 65536], P(None, 'bead', 'space')
The draws below stay inside these ranges and needn't reach their ends.
Inputs may be any that keep to these rules, and one draw needn't show every extreme that they name: `neighbours`: the row of block b holds 5 different blocks within 4 blocks of b, b itself and one block exactly 4 away among them.
All inputs are finite; a program needn't handle non-finite values.
Results may differ from the reference program's by a relative error of at most 0.0003.
Values sent between devices are 32-bit elements; how exact they have to be, the bound alone decides.
A program may use at most 64 MiB of HBM per device.

```python
import math
import jax
import jax.numpy as jnp
from jax import lax

BEADS = 32
BLOCK = 128
HALO = 4
NBR = 5
STEPS = 2
ATOMS = 65536
BLOCKS = 512


def draw_positions(key, part):
    centre_key, spread_key = jax.random.split(jax.random.fold_in(key, 11))
    extent = jnp.array([1.0, 2.0, 2.0], dtype=jnp.float32)[:, None, None]
    centre = jax.random.uniform(centre_key, (3, 1, ATOMS), jnp.float32) * extent
    spread = 0.03 * jnp.clip(jax.random.normal(spread_key, (3, BEADS, ATOMS), jnp.float32), -4.0, 4.0)
    return centre + spread


def draw_neighbours(key, part):
    span_size = 2 * HALO + 1
    candidate = jnp.arange(span_size, dtype=jnp.int32) - HALO
    blocks = jnp.arange(BLOCKS, dtype=jnp.int32)[:, None]
    target = blocks + candidate[None, :]
    in_range = (target >= 0) & (target < BLOCKS)
    random_part = jax.random.randint(jax.random.fold_in(key, 23), (BLOCKS, span_size), 0, 1 << 20, dtype=jnp.int32)
    scores = random_part * span_size + candidate[None, :] + HALO
    top_value = (1 << 20) * span_size
    lower_ok = in_range[:, :1]
    upper_ok = in_range[:, -1:]
    odd_block = blocks % 2 == 1
    pick_upper = odd_block & upper_ok | jnp.logical_not(lower_ok)
    far_pick = jnp.where(pick_upper, candidate[None, :] == HALO, candidate[None, :] == -HALO)
    scores = jnp.where(far_pick, top_value + span_size, scores)
    scores = jnp.where(candidate[None, :] == 0, top_value + 2 * span_size, scores)
    scores = jnp.where(in_range, scores, -1 - candidate[None, :] - HALO)
    chosen = lax.top_k(scores, NBR)[1]
    return jnp.take_along_axis(target, chosen, axis=1).astype(jnp.int32)


def place_ends(values, key, low, largest):
    spot = [jax.random.randint(jax.random.fold_in(key, axis), (), 0, length) for axis, length in enumerate(values.shape)]
    widest = values.shape.index(max(values.shape))
    beside = spot[:widest] + [(spot[widest] + 1) % values.shape[widest]] + spot[widest + 1:]
    return values.at[tuple(spot)].set(low).at[tuple(beside)].set(largest)


def block_scale(rng, dims, shards, smallest, largest):
    def one(axis_at, parts):
        heights = jax.random.uniform(jax.random.fold_in(jax.random.fold_in(rng, 6), axis_at), (parts,), jnp.float32, smallest / len(shards), largest / len(shards))
        return jnp.repeat(jnp.exp(heights), dims[axis_at] // parts).reshape((-1,) + (1,) * (len(dims) - axis_at - 1))

    loudness = one(*shards[0])
    for cut in shards[1:]:
        loudness = loudness * one(*cut)
    return loudness


def gaussian(stream_key, shape, width, reach, shards=(), kind=jnp.bfloat16):
    values = jax.random.normal(stream_key, shape, jnp.float32) * width
    if len(shards) > 0:
        values = block_scale(stream_key, shape, shards, -0.22, 0.18) * values
    return jnp.clip(values, min=-reach, max=reach).astype(kind)


def setup_inputs(seed: int = 0) -> dict:
    keys = jax.random.split(jax.random.key(seed), 6)
    return {
        "positions": draw_positions(jax.random.fold_in(keys[5], 71), 0),
        "momenta": gaussian(keys[1], (3, BEADS, ATOMS), 1.0, 6.0, ((1, 32), (2, 16)), jnp.float32),
        "atom_types": place_ends(jax.random.randint(keys[2], (ATOMS,), 0, 4), jax.random.fold_in(keys[2], 1), 0, 3).astype(jnp.int32),
        "neighbours": draw_neighbours(jax.random.fold_in(keys[5], 71), 0),
        "thermal_noise": gaussian(keys[4], (STEPS, 3, BEADS, ATOMS), 1.0, 6.0, ((2, 32), (3, 16)), jnp.float32),
    }


half_step = 0.025
time_step = 0.05
chain_freq = 12.0
thermal = 0.375
centroid_friction = 1.0
screening = 4.0
softening = 0.09
highest = lax.Precision.HIGHEST

def materials(atom_types):
    onehot = (atom_types[:, None] == jnp.arange(4, dtype=jnp.int32)[None, :]).astype(jnp.float32)
    charge_table = jnp.array([1.0, -1.0, 0.6, -1.4], dtype=jnp.float32)
    mass_table = jnp.array([1.0, 2.0, 3.0, 4.0], dtype=jnp.float32)
    return (lax.optimization_barrier(jnp.sum(onehot * charge_table[None, :], axis=1)), lax.optimization_barrier(jnp.sum(onehot * mass_table[None, :], axis=1)))

def mode_matrix(bead_total):
    bead_ids = jnp.arange(bead_total, dtype=jnp.float32)[:, None]
    mode_ids = jnp.arange(bead_total, dtype=jnp.int32)[None, :]
    phase_grid = 2.0 * jnp.pi * bead_ids * mode_ids.astype(jnp.float32) / bead_total
    half_mode = bead_total // 2
    plain = 1.0 / math.sqrt(bead_total)
    paired = math.sqrt(2.0 / bead_total)
    return jnp.where(mode_ids == 0, plain + 0.0 * phase_grid, jnp.where(mode_ids < half_mode, paired * jnp.cos(phase_grid), jnp.where(mode_ids == half_mode, plain * jnp.cos(phase_grid), paired * jnp.sin(phase_grid))))

def mode_tables(bead_total):
    mode_ids = jnp.arange(bead_total, dtype=jnp.float32)
    frequency = 2.0 * chain_freq * jnp.sin(jnp.pi * mode_ids / bead_total)
    angle_step = frequency * time_step
    cosine = jnp.cos(angle_step)
    sine_ratio = jnp.where(mode_ids == 0, time_step, jnp.sin(angle_step) / jnp.where(mode_ids == 0, 1.0, frequency))
    stiffness = frequency * jnp.sin(angle_step)
    friction = jnp.where(mode_ids == 0, centroid_friction, 2.0 * frequency)
    damping = jnp.exp(-friction * time_step)
    kick_scale = jnp.sqrt(1.0 - damping * damping)
    return (cosine, sine_ratio, stiffness, damping, kick_scale)

def tile_force(own_rows, tile_rows, shift_rows):
    delta_x = own_rows[0][:, None, :, None] - tile_rows[0][:, :, None, :] + shift_rows[:, :, None, None]
    delta_y = own_rows[1][:, None, :, None] - tile_rows[1][:, :, None, :]
    delta_z = own_rows[2][:, None, :, None] - tile_rows[2][:, :, None, :]
    square = delta_x * delta_x + delta_y * delta_y + delta_z * delta_z + softening
    distance = jnp.sqrt(square)
    weight = jnp.exp(-distance / screening) * (1.0 / (screening * distance) + 1.0 / square) / distance
    weight = weight * tile_rows[3][:, :, None, :]
    force_x = own_rows[3] * lax.optimization_barrier(jnp.sum(weight * delta_x, axis=(1, 3)))
    force_y = own_rows[3] * lax.optimization_barrier(jnp.sum(weight * delta_y, axis=(1, 3)))
    force_z = own_rows[3] * lax.optimization_barrier(jnp.sum(weight * delta_z, axis=(1, 3)))
    return jnp.stack([force_x, force_y, force_z])

def bead_forces(extended, first_block, lists, offsets, group_size):
    block_count = lists.shape[0]

    def group_force(group_index):
        begin_row = group_index * group_size
        own_rows = lax.dynamic_slice_in_dim(extended, first_block + begin_row, group_size, 1)
        list_rows = lax.dynamic_slice_in_dim(lists, begin_row, group_size, 0)
        shift_rows = lax.dynamic_slice_in_dim(offsets, begin_row, group_size, 0)
        tile_rows = jnp.take(extended, list_rows, axis=1)
        return tile_force(own_rows, tile_rows, shift_rows)
    result = lax.map(group_force, jnp.arange(block_count // group_size, dtype=jnp.int32))
    return jnp.transpose(result, (1, 0, 2, 3)).reshape(3, block_count * extended.shape[2])

def thermostat_and_drift(mode_coords, mode_moment, noise_now, atom_mass, tables):
    cosine, sine_ratio, stiffness, damping, kick_scale = tuple((entry[None, :, None] for entry in tables))
    mass_row = atom_mass[None, None, :]
    moment_new = damping * mode_moment + kick_scale * jnp.sqrt(thermal * mass_row) * noise_now
    next_coords = cosine * mode_coords + sine_ratio * moment_new / mass_row
    next_moment = cosine * moment_new - stiffness * mass_row * mode_coords
    return (next_coords, next_moment)

def reference(positions, momenta, atom_types, neighbours, thermal_noise):
    charge, atom_mass = materials(atom_types)
    matrix = mode_matrix(BEADS)
    tables = mode_tables(BEADS)
    offsets = (jnp.arange(BLOCKS, dtype=jnp.int32)[:, None] - neighbours).astype(jnp.float32)
    charge_blocks = charge.reshape(1, BLOCKS, BLOCK)

    def all_forces(coords):

        def one_bead(single):
            extended = jnp.concatenate([single.reshape(3, BLOCKS, BLOCK), charge_blocks], axis=0)
            return bead_forces(extended, 0, neighbours, offsets, 2)
        per_bead = lax.map(one_bead, jnp.transpose(coords, (1, 0, 2)))
        return jnp.transpose(per_bead, (1, 0, 2))
    forces_now = all_forces(positions)
    coords, moment = (positions, momenta)
    for turn_index in range(STEPS):
        moment = moment + half_step * forces_now
        mode_coords = jnp.einsum('jk,cja->cka', matrix, coords, precision=highest)
        mode_moment = jnp.einsum('jk,cja->cka', matrix, moment, precision=highest)
        next_coords, next_moment = thermostat_and_drift(mode_coords, mode_moment, thermal_noise[turn_index], atom_mass, tables)
        coords = jnp.einsum('jk,cka->cja', matrix, next_coords, precision=highest)
        moment = jnp.einsum('jk,cka->cja', matrix, next_moment, precision=highest)
        forces_now = all_forces(coords)
        moment = moment + half_step * forces_now
    return (coords, moment)
```

```python
import functools
import math

import jax
import jax.numpy as jnp
import numpy as np
from jax import lax
from jax.experimental import pallas as pl
from jax.experimental.pallas import tpu as pltpu
from jax.sharding import PartitionSpec as P

MESH = pl.DeviceIdType.MESH
F32 = jnp.float32
BF16 = jnp.bfloat16
LANES = 128
HALO = 4
NBR = 5
ROWS = 48
half_step = 0.025
time_step = 0.05
chain_freq = 12.0
thermal = 0.375
screening = 4.0
softening = 0.09
decay = math.log2(math.e) / screening
highest = lax.Precision.HIGHEST


def mode_matrix(n):
    j = np.arange(n)[:, None]
    k = np.arange(n)[None, :]
    phase = 2.0 * np.pi * j * k / n
    plain, paired = 1.0 / math.sqrt(n), math.sqrt(2.0 / n)
    return np.where(
        k == 0,
        plain,
        np.where(
            k < n // 2,
            paired * np.cos(phase),
            np.where(k == n // 2, plain * np.cos(phase), paired * np.sin(phase)),
        ),
    ).astype(np.float32)


def mode_tables(n):
    k = np.arange(n)
    w = 2.0 * chain_freq * np.sin(np.pi * k / n)
    angle = w * time_step
    ratio = np.where(k == 0, time_step, np.sin(angle) / np.where(k == 0, 1.0, w))
    friction = np.where(k == 0, 1.0, 2.0 * w)
    damping = np.exp(-friction * time_step)
    kick = np.sqrt(1.0 - damping * damping)
    tables = np.stack([np.cos(angle), ratio, w * np.sin(angle), damping, kick])
    return np.repeat(tables[:, :, None], LANES, axis=2).astype(np.float32)


def shift_table():
    parts = {0: (0, 0), 1: (1, 0), 2: (2, 0), 3: (2, 1), 4: (4, 0)}
    table = np.ones((2 * HALO + 1, ROWS), np.float32)
    for s in range(-HALO, HALO + 1):
        sign = -1 if s < 0 else 1
        one, two = parts[abs(s)]
        table[s + HALO, 27] = s * s
        table[s + HALO, 28:32] = -2 * s
        table[s + HALO, 32:36] = sign * one
        table[s + HALO, 36:40] = sign * two
    return np.repeat(table[:, :, None], LANES, axis=2)


def charge_of(types):
    return jnp.where(
        types == 0, 1.0, jnp.where(types == 1, -1.0, jnp.where(types == 2, 0.6, -1.4))
    ).astype(F32)


def three(v):
    high = v.astype(BF16).astype(F32)
    rest = v - high
    mid = rest.astype(BF16).astype(F32)
    return high, mid, rest - mid


def kernel(
    nb,
    ns,
    lists,
    x_ref,
    p_ref,
    noise_ref,
    types_ref,
    mult_ref,
    to_mode,
    to_bead,
    tab_ref,
    x_out,
    p_out,
    xin,
    pin,
    nin,
    ext,
    extq,
    fout,
    fin,
    xs,
    ps,
    pbuf,
    modes,
    fe,
    fb,
    fa,
    s_in,
    r_in,
    s_h,
    r_h,
    s_f,
    r_f,
    s_x,
    r_x,
    s_xh,
    r_xh,
    s_p,
    r_p,
):
    me = lax.axis_index("bead")
    dom = lax.axis_index("space")
    first = dom * nb
    lower, upper = dom > 0, dom < ns - 1

    def lanes(block):
        return pl.ds(pl.multiple_of(block * LANES, LANES), LANES)

    def remote(src, dst, send, recv, bead, space):
        return pltpu.make_async_remote_copy(
            src_ref=src,
            dst_ref=dst,
            send_sem=send,
            recv_sem=recv,
            device_id=(bead, space),
            device_id_type=MESH,
        )

    def arrived(ref, sem):
        pltpu.make_async_copy(ref, ref, sem).wait()

    def others(body):
        def step(i, carry):
            body(lax.rem(me + i, nb))
            return carry

        lax.fori_loop(1, nb, step, 0)

    def loop(begin, end, body):
        def step(i, carry):
            body(i)
            return carry

        lax.fori_loop(begin, end, step, 0)

    barrier = pltpu.get_barrier_semaphore()

    def greet(bead, space):
        pl.semaphore_signal(barrier, inc=1, device_id=(bead, space), device_id_type=MESH)

    others(lambda t: greet(t, dom))

    @pl.when(lower)
    def _():
        loop(nb - HALO, nb, lambda t: greet(t, dom - 1))

        @pl.when(me < nb - HALO)
        def _():
            greet(me, dom - 1)

    @pl.when(upper)
    def _():
        loop(0, HALO, lambda t: greet(t, dom + 1))

        @pl.when(me >= HALO)
        def _():
            greet(me, dom + 1)

    row8 = lax.broadcasted_iota(jnp.int32, (4, LANES), 0)
    last = row8 == 3
    ones4 = jnp.ones((4, LANES), F32)
    zero4 = jnp.zeros((4, LANES), F32)
    minus4 = jnp.where(last, 0.0, -1.0)

    def centred(turn, n):
        return [ext[turn, n, c] - 1.0 for c in range(3)]

    def features(turn, n, own):
        x, y, z = centred(turn, n)
        q = extq[n]
        norm = x * x + y * y + z * z
        v = jnp.concatenate(
            [x, y, z, norm, norm + softening, norm, norm, norm], axis=0
        )
        high, mid, low = three(v)
        h4, m4, l4 = high[0:4], mid[0:4], low[0:4]
        hx, mx, lx = high[0:1], mid[0:1], low[0:1]
        split_x = jnp.concatenate([hx, mx, lx, jnp.zeros_like(hx)], axis=0)
        left = jnp.concatenate(
            [h4, m4, l4, h4, m4, h4, ones4, split_x, minus4, minus4, zero4, zero4],
            axis=0,
        )
        fe[n] = left.T.astype(BF16)
        heavy = jnp.concatenate([x, y, z, jnp.ones_like(x)], axis=0) * q
        qh, qm, ql = three(heavy)
        fb[n] = jnp.concatenate([qh, qm, ql, zero4], axis=0).astype(BF16)
        if own:
            ah = jnp.where(last, 1.0, -2.0 * h4)
            am = jnp.where(last, 0.0, -2.0 * m4)
            al = jnp.where(last, 0.0, -2.0 * l4)
            square = jnp.concatenate(
                [high[4:5], mid[4:5], low[4:5], jnp.ones_like(x)], axis=0
            )
            unit = jnp.where(last, 0.0, 1.0)
            twice = -2.0 * split_x
            right = jnp.concatenate(
                [ah, ah, ah, am, am, al, square, unit, twice, twice, zero4, zero4],
                axis=0,
            )
            fa[n - HALO] = right.astype(BF16)

    def force(turn, b):
        base = fa[b]
        total = jnp.zeros((16, LANES), F32)
        moved = jnp.zeros((16, LANES), F32)
        for m in range(NBR):
            listed = lists[b, m]
            n = jnp.clip(listed - first + HALO, 0, nb + 2 * HALO - 1)
            s = jnp.clip(first + b - listed, -HALO, HALO)
            right = base * mult_ref[s + HALO]
            square = jnp.dot(fe[n], right, preferred_element_type=F32)
            r = lax.rsqrt(square)
            weight = jnp.exp2((square * r) * (-decay)) * ((r * r) * (r + 0.25))
            high = weight.astype(BF16)
            low = (weight - high.astype(F32)).astype(BF16)
            left = fb[n]
            part = jnp.dot(
                jnp.concatenate([left, left], axis=1),
                jnp.concatenate([high, low], axis=0),
                preferred_element_type=F32,
            )
            total = total + part
            moved = moved + s.astype(F32) * part
        sums = total[0:4] + total[4:8] + total[8:12]
        shifted = moved[3:4] + moved[7:8] + moved[11:12]
        x, y, z = centred(turn, b + HALO)
        q = extq[b + HALO]
        plain = sums[3:4]
        fx = q * (x * plain + shifted - sums[0:1])
        fy = q * (y * plain - sums[1:2])
        fz = q * (z * plain - sums[2:3])
        return fx, fy, fz

    def send_force(turn, b):
        fx, fy, fz = force(turn, b)
        fout[turn, b, 0] = fx
        fout[turn, b, 1] = fy
        fout[turn, b, 2] = fz

        @pl.when(b != me)
        def _():
            remote(fout.at[turn, b], fin.at[turn, me], s_f.at[turn], r_f.at[turn], b, dom).start()

    def gather_force(turn):
        fin[turn, me] = fout[turn, me]
        arrived(fin.at[turn, pl.ds(0, nb - 1)], r_f.at[turn])

    def load_own(b):
        ext[0, HALO + b] = x_ref[:, :, lanes(b)]
        extq[HALO + b] = charge_of(types_ref[pl.ds(b, 1), :])

    loop(0, nb, load_own)

    @pl.when(jnp.logical_not(lower))
    def _():
        for t in range(3):
            ext[t, 0:HALO] = jnp.zeros((HALO, 3, 1, LANES), F32)
        extq[0:HALO] = jnp.zeros((HALO, 1, LANES), F32)

    @pl.when(jnp.logical_not(upper))
    def _():
        for t in range(3):
            ext[t, nb + HALO : nb + 2 * HALO] = jnp.zeros((HALO, 3, 1, LANES), F32)
        extq[nb + HALO : nb + 2 * HALO] = jnp.zeros((HALO, 1, LANES), F32)

    loop(HALO, nb + HALO, lambda n: features(0, n, True))

    senders = (
        nb
        - 1
        + jnp.where(lower, jnp.where(me < HALO, nb, 1), 0)
        + jnp.where(upper, jnp.where(me >= nb - HALO, nb, 1), 0)
    )
    pl.semaphore_wait(barrier, senders)

    low_edge, low_halo = pl.ds(HALO, HALO), pl.ds(0, HALO)
    high_edge, high_halo = pl.ds(nb, HALO), pl.ds(nb + HALO, HALO)

    def down():
        return [
            remote(ext.at[0, low_edge], ext.at[0, high_halo], s_h.at[0], r_h.at[0], me, dom - 1),
            remote(extq.at[low_edge], extq.at[high_halo], s_h.at[1], r_h.at[1], me, dom - 1),
        ]

    def up():
        return [
            remote(ext.at[0, high_edge], ext.at[0, low_halo], s_h.at[2], r_h.at[2], me, dom + 1),
            remote(extq.at[high_edge], extq.at[low_halo], s_h.at[3], r_h.at[3], me, dom + 1),
        ]

    @pl.when(lower)
    def _():
        for copy in down():
            copy.start()

    @pl.when(upper)
    def _():
        for copy in up():
            copy.start()

    def send_start(t):
        remote(x_ref.at[:, :, lanes(t)], xin.at[me], s_in.at[0], r_in.at[0], t, dom).start()
        remote(p_ref.at[:, :, lanes(t)], pin.at[me], s_in.at[1], r_in.at[1], t, dom).start()
        remote(noise_ref.at[0, :, :, lanes(t)], nin.at[0, me], s_in.at[2], r_in.at[2], t, dom).start()

    def send_noise(t):
        remote(noise_ref.at[1, :, :, lanes(t)], nin.at[1, me], s_in.at[3], r_in.at[3], t, dom).start()

    others(send_start)
    xin[me] = x_ref[:, :, lanes(me)]
    pin[me] = p_ref[:, :, lanes(me)]
    nin[0, me] = noise_ref[0, :, :, lanes(me)]
    nin[1, me] = noise_ref[1, :, :, lanes(me)]

    inner = nb - 2 * HALO
    if inner > 0:
        loop(0, inner, lambda i: send_force(0, HALO + lax.rem(me + i, inner)))

    @pl.when(upper)
    def _():
        arrived(ext.at[0, high_halo], r_h.at[0])
        arrived(extq.at[high_halo], r_h.at[1])

    @pl.when(lower)
    def _():
        arrived(ext.at[0, low_halo], r_h.at[2])
        arrived(extq.at[low_halo], r_h.at[3])

    loop(0, HALO, lambda n: features(0, n, False))
    loop(nb + HALO, nb + 2 * HALO, lambda n: features(0, n, False))

    def edge(i):
        spot = lax.rem(me + i, 2 * HALO)
        send_force(0, jnp.where(spot < HALO, spot, spot + inner))

    loop(0, 2 * HALO, edge)
    others(send_noise)

    mass = (types_ref[pl.ds(me, 1), :] + 1).astype(F32)
    width = jnp.sqrt(thermal * mass)
    inverse = 1.0 / mass
    cosine, ratio, stiffness, damping, kick = [tab_ref[i] for i in range(5)]

    def component(ref, lead, c):
        return jnp.concatenate([ref[(*lead, j, c)] for j in range(nb)], axis=0)

    def times(matrix, parts):
        whole = jnp.concatenate(parts, axis=1)
        out = jnp.dot(matrix[...], whole, precision=highest, preferred_element_type=F32)
        return [out[:, LANES * i : LANES * (i + 1)] for i in range(len(parts))]

    def drift(turn, mode_x, mode_p):
        next_x, next_p = [], []
        for c in range(3):
            noise = component(nin, (turn,), c)
            p_new = damping * mode_p[c] + kick * width * noise
            next_x.append(cosine * mode_x[c] + ratio * p_new * inverse)
            next_p.append(cosine * p_new - stiffness * mass * mode_x[c])
        return next_x, next_p

    def spread(ref, lead, parts):
        for c in range(3):
            for j in range(nb):
                ref[(*lead, j, c)] = parts[c][j : j + 1]

    def send_coords(turn):
        others(
            lambda t: remote(
                xs.at[turn - 1, t],
                ext.at[turn, HALO + me],
                s_x.at[turn - 1],
                r_x.at[turn - 1],
                t,
                dom,
            ).start()
        )

        @pl.when(jnp.logical_and(lower, me < HALO))
        def _():
            loop(
                0,
                nb,
                lambda t: remote(
                    xs.at[turn - 1, lax.rem(me + t, nb)],
                    ext.at[turn, nb + HALO + me],
                    s_xh.at[turn - 1],
                    r_xh.at[turn - 1, 0],
                    lax.rem(me + t, nb),
                    dom - 1,
                ).start(),
            )

        @pl.when(jnp.logical_and(upper, me >= nb - HALO))
        def _():
            loop(
                0,
                nb,
                lambda t: remote(
                    xs.at[turn - 1, lax.rem(me + t, nb)],
                    ext.at[turn, me - (nb - HALO)],
                    s_xh.at[turn - 1],
                    r_xh.at[turn - 1, 1],
                    lax.rem(me + t, nb),
                    dom + 1,
                ).start(),
            )

        ext[turn, HALO + me] = xs[turn - 1, me]

    def gather_coords(turn):
        arrived(ext.at[turn, pl.ds(0, nb - 1)], r_x.at[turn - 1])

        @pl.when(upper)
        def _():
            arrived(ext.at[turn, pl.ds(0, HALO)], r_xh.at[turn - 1, 0])

        @pl.when(lower)
        def _():
            arrived(ext.at[turn, pl.ds(0, HALO)], r_xh.at[turn - 1, 1])

    def all_features(turn):
        loop(HALO, nb + HALO, lambda n: features(turn, n, True))
        loop(0, HALO, lambda n: features(turn, n, False))
        loop(nb + HALO, nb + 2 * HALO, lambda n: features(turn, n, False))

    some = pl.ds(0, nb - 1)
    arrived(xin.at[some], r_in.at[0])
    arrived(pin.at[some], r_in.at[1])
    arrived(nin.at[0, some], r_in.at[2])
    gather_force(0)
    parts = [component(xin, (), c) for c in range(3)] + [
        component(pin, (), c) + half_step * component(fin, (0,), c) for c in range(3)
    ]
    parts = times(to_mode, parts)
    mode_x, mode_p = drift(0, parts[:3], parts[3:])
    spread(xs, (0,), times(to_bead, mode_x))
    send_coords(1)
    for c in range(3):
        modes[c] = mode_x[c]
        modes[3 + c] = mode_p[c]

    gather_coords(1)
    all_features(1)
    loop(0, nb, lambda i: send_force(1, lax.rem(me + i, nb)))
    arrived(nin.at[1, some], r_in.at[3])
    gather_force(1)
    kicks = times(to_mode, [component(fin, (1,), c) for c in range(3)])
    mode_x, mode_p = drift(
        1,
        [modes[c] for c in range(3)],
        [modes[3 + c] + 2.0 * half_step * kicks[c] for c in range(3)],
    )
    spread(xs, (1,), times(to_bead, mode_x))
    send_coords(2)
    spread(ps, (), times(to_bead, mode_p))
    others(lambda t: remote(ps.at[t], pbuf.at[me], s_p, r_p, t, dom).start())
    pbuf[me] = ps[me]

    gather_coords(2)
    all_features(2)
    arrived(pbuf.at[some], r_p)

    def finish(b):
        for c, f in enumerate(force(2, b)):
            x_out[c, :, lanes(b)] = ext[2, HALO + b, c]
            p_out[c, :, lanes(b)] = pbuf[b, c] + half_step * f

    loop(0, nb, finish)

    arrived(xin.at[some], s_in.at[0])
    arrived(pin.at[some], s_in.at[1])
    arrived(nin.at[0, some], s_in.at[2])
    arrived(nin.at[1, some], s_in.at[3])
    for turn in range(2):
        arrived(fin.at[turn, some], s_f.at[turn])
        arrived(xs.at[turn, some], s_x.at[turn])

        @pl.when(jnp.logical_or(jnp.logical_and(lower, me < HALO), jnp.logical_and(upper, me >= nb - HALO)))
        def _():
            arrived(xs.at[turn], s_xh.at[turn])

    arrived(ps.at[some], s_p)

    @pl.when(lower)
    def _():
        for copy in down():
            copy.wait_send()

    @pl.when(upper)
    def _():
        for copy in up():
            copy.wait_send()


def solution(mesh):
    nb, ns = mesh.shape["bead"], mesh.shape["space"]

    def body(positions, momenta, atom_types, neighbours, thermal_noise):
        matrix = mode_matrix(nb)
        vmem = pl.BlockSpec(memory_space=pltpu.VMEM)
        piece = (3, 1, LANES)
        dma = pltpu.SemaphoreType.DMA
        return pl.pallas_call(
            functools.partial(kernel, nb, ns),
            out_shape=(
                jax.ShapeDtypeStruct(positions.shape, F32),
                jax.ShapeDtypeStruct(momenta.shape, F32),
            ),
            in_specs=[pl.BlockSpec(memory_space=pltpu.SMEM)] + [vmem] * 8,
            out_specs=(vmem, vmem),
            scratch_shapes=[
                pltpu.VMEM((nb, *piece), F32),
                pltpu.VMEM((nb, *piece), F32),
                pltpu.VMEM((2, nb, *piece), F32),
                pltpu.VMEM((3, nb + 2 * HALO, *piece), F32),
                pltpu.VMEM((nb + 2 * HALO, 1, LANES), F32),
                pltpu.VMEM((2, nb, *piece), F32),
                pltpu.VMEM((2, nb, *piece), F32),
                pltpu.VMEM((2, nb, *piece), F32),
                pltpu.VMEM((nb, *piece), F32),
                pltpu.VMEM((nb, *piece), F32),
                pltpu.VMEM((6, nb, LANES), F32),
                pltpu.VMEM((nb + 2 * HALO, LANES, ROWS), BF16),
                pltpu.VMEM((nb + 2 * HALO, 16, LANES), BF16),
                pltpu.VMEM((nb, ROWS, LANES), BF16),
                dma((4,)),
                dma((4,)),
                dma((4,)),
                dma((4,)),
                dma((2,)),
                dma((2,)),
                dma((2,)),
                dma((2,)),
                dma((2,)),
                dma((2, 2)),
                dma,
                dma,
            ],
            compiler_params=pltpu.CompilerParams(
                collective_id=0, has_side_effects=True, vmem_limit_bytes=32 * 1024 * 1024
            ),
            name="path_integral_steps",
        )(
            neighbours,
            positions,
            momenta,
            thermal_noise,
            atom_types.reshape(nb, LANES),
            jnp.asarray(shift_table(), BF16),
            jnp.asarray(matrix.T.copy()),
            jnp.asarray(matrix),
            jnp.asarray(mode_tables(nb)),
        )

    spec = P(None, "bead", "space")
    return jax.shard_map(
        body,
        mesh=mesh,
        in_specs=(spec, spec, P("space"), P("space", None), P(None, None, "bead", "space")),
        out_specs=(spec, spec),
        check_vma=False,
    )
```

```python
import functools
import math

import jax
import jax.numpy as jnp
import numpy as np
from jax import lax
from jax.experimental import pallas as pl
from jax.experimental.pallas import tpu as pltpu
from jax.sharding import PartitionSpec as P

MESH = pl.DeviceIdType.MESH
F32 = jnp.float32
BF16 = jnp.bfloat16
LANES = 128
HALO = 4
NBR = 5
ROWS = 48
half_step = 0.025
time_step = 0.05
chain_freq = 12.0
thermal = 0.375
screening = 4.0
softening = 0.09
decay = math.log2(math.e) / screening
highest = lax.Precision.HIGHEST


def mode_matrix(n):
    j = np.arange(n)[:, None]
    k = np.arange(n)[None, :]
    phase = 2.0 * np.pi * j * k / n
    plain, paired = 1.0 / math.sqrt(n), math.sqrt(2.0 / n)
    return np.where(
        k == 0,
        plain,
        np.where(
            k < n // 2,
            paired * np.cos(phase),
            np.where(k == n // 2, plain * np.cos(phase), paired * np.sin(phase)),
        ),
    ).astype(np.float32)


def mode_tables(n):
    k = np.arange(n)
    w = 2.0 * chain_freq * np.sin(np.pi * k / n)
    angle = w * time_step
    ratio = np.where(k == 0, time_step, np.sin(angle) / np.where(k == 0, 1.0, w))
    friction = np.where(k == 0, 1.0, 2.0 * w)
    damping = np.exp(-friction * time_step)
    kick = np.sqrt(1.0 - damping * damping)
    tables = np.stack([np.cos(angle), ratio, w * np.sin(angle), damping, kick])
    return np.repeat(tables[:, :, None], LANES, axis=2).astype(np.float32)


def shift_table():
    parts = {0: (0, 0), 1: (1, 0), 2: (2, 0), 3: (2, 1), 4: (4, 0)}
    table = np.ones((2 * HALO + 1, ROWS), np.float32)
    for s in range(-HALO, HALO + 1):
        sign = -1 if s < 0 else 1
        one, two = parts[abs(s)]
        table[s + HALO, 27] = s * s
        table[s + HALO, 28:32] = -2 * s
        table[s + HALO, 32:36] = sign * one
        table[s + HALO, 36:40] = sign * two
    return np.repeat(table[:, :, None], LANES, axis=2)


def charge_of(types):
    return jnp.where(
        types == 0, 1.0, jnp.where(types == 1, -1.0, jnp.where(types == 2, 0.6, -1.4))
    ).astype(F32)


def three(v):
    high = v.astype(BF16).astype(F32)
    rest = v - high
    mid = rest.astype(BF16).astype(F32)
    return high, mid, rest - mid


def kernel(
    nb,
    ns,
    lists,
    x_hbm,
    p_hbm,
    noise_hbm,
    types_hbm,
    mult_hbm,
    to_mode_hbm,
    to_bead_hbm,
    tab_hbm,
    x_out,
    p_out,
    x_ref,
    types_ref,
    mult_ref,
    to_mode,
    to_bead,
    tab_ref,
    xin,
    pin,
    nin,
    ext,
    extq,
    fout,
    fin,
    xs,
    ps,
    pbuf,
    modes,
    fe,
    fb,
    fa,
    s_in,
    r_in,
    s_h,
    r_h,
    s_f,
    r_f,
    s_x,
    r_x,
    s_xh,
    r_xh,
    s_p,
    r_p,
    s_own,
    even,
    odd,
):
    me = lax.axis_index("bead")
    dom = lax.axis_index("space")
    first = dom * nb
    lower, upper = dom > 0, dom < ns - 1

    def lanes(block):
        return pl.ds(pl.multiple_of(block * LANES, LANES), LANES)

    def remote(src, dst, send, recv, bead, space):
        return pltpu.make_async_remote_copy(
            src_ref=src,
            dst_ref=dst,
            send_sem=send,
            recv_sem=recv,
            device_id=(bead, space),
            device_id_type=MESH,
        )

    def arrived(ref, sem):
        pltpu.make_async_copy(ref, ref, sem).wait()

    def others(body):
        def step(i, carry):
            body(lax.rem(me + i, nb))
            return carry

        lax.fori_loop(1, nb, step, 0)

    def loop(begin, end, body):
        def step(i, carry):
            body(i)
            return carry

        lax.fori_loop(begin, end, step, 0)

    staged = [
        pltpu.make_async_copy(src, dst, s_own.at[i])
        for i, (src, dst) in enumerate(
            [
                (x_hbm, x_ref),
                (types_hbm, types_ref),
                (mult_hbm, mult_ref),
                (to_mode_hbm, to_mode),
                (to_bead_hbm, to_bead),
                (tab_hbm, tab_ref),
                (p_hbm.at[:, :, lanes(me)], pin.at[me]),
                (noise_hbm.at[0, :, :, lanes(me)], nin.at[0, me]),
                (noise_hbm.at[1, :, :, lanes(me)], nin.at[1, me]),
            ]
        )
    ]
    for copy in staged:
        copy.start()

    barrier = pltpu.get_barrier_semaphore()

    def greet(bead, space):
        pl.semaphore_signal(barrier, inc=1, device_id=(bead, space), device_id_type=MESH)

    others(lambda t: greet(t, dom))

    @pl.when(lower)
    def _():
        loop(nb - HALO, nb, lambda t: greet(t, dom - 1))

        @pl.when(me < nb - HALO)
        def _():
            greet(me, dom - 1)

    @pl.when(upper)
    def _():
        loop(0, HALO, lambda t: greet(t, dom + 1))

        @pl.when(me >= HALO)
        def _():
            greet(me, dom + 1)

    row8 = lax.broadcasted_iota(jnp.int32, (4, LANES), 0)
    last = row8 == 3
    ones4 = jnp.ones((4, LANES), F32)
    zero4 = jnp.zeros((4, LANES), F32)
    minus4 = jnp.where(last, 0.0, -1.0)

    def centred(turn, n):
        return [ext[turn, n, c] - 1.0 for c in range(3)]

    def features(turn, begin, count, own):
        group = 4

        def several(i):
            done = [one_features(turn, begin + group * i + k, own) for k in range(group)]
            for k, (left, heavy, right) in enumerate(done):
                n = begin + group * i + k
                fe[n] = left
                fb[n] = heavy
                if own:
                    fa[n - HALO] = right

        loop(0, count // group, several)

    def one_features(turn, n, own):
        right = None
        x, y, z = centred(turn, n)
        q = extq[n]
        norm = x * x + y * y + z * z
        v = jnp.concatenate(
            [x, y, z, norm, norm + softening, norm, norm, norm], axis=0
        )
        high, mid, low = three(v)
        h4, m4, l4 = high[0:4], mid[0:4], low[0:4]
        hx, mx, lx = high[0:1], mid[0:1], low[0:1]
        split_x = jnp.concatenate([hx, mx, lx, jnp.zeros_like(hx)], axis=0)
        left = jnp.concatenate(
            [h4, m4, l4, h4, m4, h4, ones4, split_x, minus4, minus4, zero4, zero4],
            axis=0,
        )
        heavy = jnp.concatenate([x, y, z, jnp.ones_like(x)], axis=0) * q
        qh, qm, ql = three(heavy)
        heavy = jnp.concatenate([qh, qm, ql, zero4], axis=0).astype(BF16)
        if own:
            ah = jnp.where(last, 1.0, -2.0 * h4)
            am = jnp.where(last, 0.0, -2.0 * m4)
            al = jnp.where(last, 0.0, -2.0 * l4)
            square = jnp.concatenate(
                [high[4:5], mid[4:5], low[4:5], jnp.ones_like(x)], axis=0
            )
            unit = jnp.where(last, 0.0, 1.0)
            twice = -2.0 * split_x
            right = jnp.concatenate(
                [ah, ah, ah, am, am, al, square, unit, twice, twice, zero4, zero4],
                axis=0,
            )
            right = right.astype(BF16)
        return left.T.astype(BF16), heavy, right

    def squares(b, ref):
        base = fa[b]
        for m in range(NBR):
            listed = lists[m, b]
            n = jnp.clip(listed - first + HALO, 0, nb + 2 * HALO - 1)
            s = jnp.clip(first + b - listed, -HALO, HALO)
            right = base * mult_ref[s + HALO]
            ref[m] = jnp.dot(fe[n], right, preferred_element_type=F32)

    def force(turn, b, ref):
        total = jnp.zeros((16, LANES), F32)
        moved = jnp.zeros((16, LANES), F32)
        for m in range(NBR):
            listed = lists[m, b]
            n = jnp.clip(listed - first + HALO, 0, nb + 2 * HALO - 1)
            s = jnp.clip(first + b - listed, -HALO, HALO)
            square = ref[m]
            r = lax.rsqrt(square)
            weight = jnp.exp2((square * r) * (-decay)) * ((r * r) * (r + 0.25))
            high = weight.astype(BF16)
            low = (weight - high.astype(F32)).astype(BF16)
            left = fb[n]
            part = jnp.dot(
                jnp.concatenate([left, left], axis=1),
                jnp.concatenate([high, low], axis=0),
                preferred_element_type=F32,
            )
            total = total + part
            moved = moved + s.astype(F32) * part
        sums = total[0:4] + total[4:8] + total[8:12]
        shifted = moved[3:4] + moved[7:8] + moved[11:12]
        x, y, z = centred(turn, b + HALO)
        q = extq[b + HALO]
        plain = sums[3:4]
        fx = q * (x * plain + shifted - sums[0:1])
        fy = q * (y * plain - sums[1:2])
        fz = q * (z * plain - sums[2:3])
        return fx, fy, fz

    def forces(turn, count, block_of, take, beside=None):
        squares(block_of(0), even)
        group = 4 if count % 4 == 0 else 2

        def several(i):
            blocks = [block_of(lax.rem(group * i + k, count)) for k in range(group + 1)]
            done = []
            for k in range(group):
                here, there = (odd, even) if k % 2 else (even, odd)
                squares(blocks[k + 1], there)
                done.append((blocks[k], force(turn, blocks[k], here)))
            take(done)
            if beside is not None:
                beside(i)

        loop(0, count // group, several)

    def keep_force(turn):
        def take(done):
            for b, parts in done:
                for c in range(3):
                    fout[turn, b, c] = parts[c]

        return take

    def send_force(turn, b):
        @pl.when(b != me)
        def _():
            remote(fout.at[turn, b], fin.at[turn, me], s_f.at[turn], r_f.at[turn], b, dom).start()

    def send_forces(turn):
        def take(done):
            keep_force(turn)(done)
            for b, _ in done:
                send_force(turn, b)

        return take

    def gather_force(turn):
        fin[turn, me] = fout[turn, me]
        arrived(fin.at[turn, pl.ds(0, nb - 1)], r_f.at[turn])

    def load_own(b):
        ext[0, HALO + b] = x_ref[:, :, lanes(b)]
        extq[HALO + b] = charge_of(types_ref[pl.ds(b, 1), :])

    staged[0].wait()
    staged[1].wait()
    loop(0, nb, load_own)

    @pl.when(jnp.logical_not(lower))
    def _():
        for t in range(3):
            ext[t, 0:HALO] = jnp.zeros((HALO, 3, 1, LANES), F32)
        extq[0:HALO] = jnp.zeros((HALO, 1, LANES), F32)

    @pl.when(jnp.logical_not(upper))
    def _():
        for t in range(3):
            ext[t, nb + HALO : nb + 2 * HALO] = jnp.zeros((HALO, 3, 1, LANES), F32)
        extq[nb + HALO : nb + 2 * HALO] = jnp.zeros((HALO, 1, LANES), F32)

    features(0, HALO, nb, True)
    staged[2].wait()
    inner = nb - 2 * HALO
    early = inner // 6 * 2
    late = inner - early

    def inner_block(i):
        return HALO + lax.rem(me + i, inner)

    if early > 0:
        forces(0, early, inner_block, keep_force(0))

    senders = (
        nb
        - 1
        + jnp.where(lower, jnp.where(me < HALO, nb, 1), 0)
        + jnp.where(upper, jnp.where(me >= nb - HALO, nb, 1), 0)
    )
    pl.semaphore_wait(barrier, senders)

    low_edge, low_halo = pl.ds(HALO, HALO), pl.ds(0, HALO)
    high_edge, high_halo = pl.ds(nb, HALO), pl.ds(nb + HALO, HALO)

    def down():
        return [
            remote(ext.at[0, low_edge], ext.at[0, high_halo], s_h.at[0], r_h.at[0], me, dom - 1),
            remote(extq.at[low_edge], extq.at[high_halo], s_h.at[1], r_h.at[1], me, dom - 1),
        ]

    def up():
        return [
            remote(ext.at[0, high_edge], ext.at[0, low_halo], s_h.at[2], r_h.at[2], me, dom + 1),
            remote(extq.at[high_edge], extq.at[low_halo], s_h.at[3], r_h.at[3], me, dom + 1),
        ]

    @pl.when(lower)
    def _():
        for copy in down():
            copy.start()

    @pl.when(upper)
    def _():
        for copy in up():
            copy.start()

    def send_start(t):
        remote(x_hbm.at[:, :, lanes(t)], xin.at[me], s_in.at[0], r_in.at[0], t, dom).start()
        remote(p_hbm.at[:, :, lanes(t)], pin.at[me], s_in.at[1], r_in.at[1], t, dom).start()
        remote(noise_hbm.at[0, :, :, lanes(t)], nin.at[0, me], s_in.at[2], r_in.at[2], t, dom).start()

    def send_noise(t):
        remote(noise_hbm.at[1, :, :, lanes(t)], nin.at[1, me], s_in.at[3], r_in.at[3], t, dom).start()

    rounds = max(late // (4 if late % 4 == 0 else 2), 1)
    beside = (nb - 1) // rounds if late > 0 else 0

    def send_started(begin, end):
        loop(begin, end, lambda i: send_start(lax.rem(me + i, nb)))

    xin[me] = x_ref[:, :, lanes(me)]
    send_started(1 + beside * rounds, nb)
    if early > 0:
        loop(0, early, lambda i: send_force(0, inner_block(i)))
    if late > 0:

        def send_beside(i):
            for k in range(beside):
                send_start(lax.rem(me + 1 + beside * i + k, nb))

        forces(0, late, lambda i: inner_block(early + i), send_forces(0), send_beside)

    @pl.when(upper)
    def _():
        arrived(ext.at[0, high_halo], r_h.at[0])
        arrived(extq.at[high_halo], r_h.at[1])

    @pl.when(lower)
    def _():
        arrived(ext.at[0, low_halo], r_h.at[2])
        arrived(extq.at[low_halo], r_h.at[3])

    features(0, 0, HALO, False)
    features(0, nb + HALO, HALO, False)

    def edge(i):
        spot = lax.rem(me + i, 2 * HALO)
        return jnp.where(spot < HALO, spot, spot + inner)

    forces(0, 2 * HALO, edge, send_forces(0))
    others(send_noise)

    for copy in staged[3:]:
        copy.wait()
    mass = (types_ref[pl.ds(me, 1), :] + 1).astype(F32)
    width = jnp.sqrt(thermal * mass)
    inverse = 1.0 / mass
    cosine, ratio, stiffness, damping, kick = [tab_ref[i] for i in range(5)]

    def component(ref, lead, c):
        return jnp.concatenate([ref[(*lead, j, c)] for j in range(nb)], axis=0)

    def times(matrix, parts):
        whole = jnp.concatenate(parts, axis=1)
        out = jnp.dot(matrix[...], whole, precision=highest, preferred_element_type=F32)
        return [out[:, LANES * i : LANES * (i + 1)] for i in range(len(parts))]

    def drift(turn, mode_x, mode_p):
        next_x, next_p = [], []
        for c in range(3):
            noise = component(nin, (turn,), c)
            p_new = damping * mode_p[c] + kick * width * noise
            next_x.append(cosine * mode_x[c] + ratio * p_new * inverse)
            next_p.append(cosine * p_new - stiffness * mass * mode_x[c])
        return next_x, next_p

    def spread(ref, lead, parts):
        for c in range(3):
            for j in range(nb):
                ref[(*lead, j, c)] = parts[c][j : j + 1]

    def send_coords(turn):
        others(
            lambda t: remote(
                xs.at[turn - 1, t],
                ext.at[turn, HALO + me],
                s_x.at[turn - 1],
                r_x.at[turn - 1],
                t,
                dom,
            ).start()
        )

        @pl.when(jnp.logical_and(lower, me < HALO))
        def _():
            loop(
                0,
                nb,
                lambda t: remote(
                    xs.at[turn - 1, lax.rem(me + t, nb)],
                    ext.at[turn, nb + HALO + me],
                    s_xh.at[turn - 1],
                    r_xh.at[turn - 1, 0],
                    lax.rem(me + t, nb),
                    dom - 1,
                ).start(),
            )

        @pl.when(jnp.logical_and(upper, me >= nb - HALO))
        def _():
            loop(
                0,
                nb,
                lambda t: remote(
                    xs.at[turn - 1, lax.rem(me + t, nb)],
                    ext.at[turn, me - (nb - HALO)],
                    s_xh.at[turn - 1],
                    r_xh.at[turn - 1, 1],
                    lax.rem(me + t, nb),
                    dom + 1,
                ).start(),
            )

        ext[turn, HALO + me] = xs[turn - 1, me]

    def gather_coords(turn):
        arrived(ext.at[turn, pl.ds(0, nb - 1)], r_x.at[turn - 1])

        @pl.when(upper)
        def _():
            arrived(ext.at[turn, pl.ds(0, HALO)], r_xh.at[turn - 1, 0])

        @pl.when(lower)
        def _():
            arrived(ext.at[turn, pl.ds(0, HALO)], r_xh.at[turn - 1, 1])

    def all_features(turn):
        features(turn, HALO, nb, True)
        features(turn, 0, HALO, False)
        features(turn, nb + HALO, HALO, False)

    some = pl.ds(0, nb - 1)
    arrived(xin.at[some], r_in.at[0])
    arrived(pin.at[some], r_in.at[1])
    arrived(nin.at[0, some], r_in.at[2])
    parts = [component(xin, (), c) for c in range(3)] + [component(pin, (), c) for c in range(3)]
    parts = times(to_mode, parts)
    for c in range(6):
        modes[c] = parts[c]
    gather_force(0)
    kicks = times(to_mode, [component(fin, (0,), c) for c in range(3)])
    mode_x, mode_p = drift(
        0,
        [modes[c] for c in range(3)],
        [modes[3 + c] + half_step * kicks[c] for c in range(3)],
    )
    spread(xs, (0,), times(to_bead, mode_x))
    send_coords(1)
    for c in range(3):
        modes[c] = mode_x[c]
        modes[3 + c] = mode_p[c]

    gather_coords(1)
    all_features(1)
    forces(1, nb, lambda i: lax.rem(me + i, nb), send_forces(1))
    arrived(nin.at[1, some], r_in.at[3])
    gather_force(1)
    kicks = times(to_mode, [component(fin, (1,), c) for c in range(3)])
    mode_x, mode_p = drift(
        1,
        [modes[c] for c in range(3)],
        [modes[3 + c] + 2.0 * half_step * kicks[c] for c in range(3)],
    )
    spread(xs, (1,), times(to_bead, mode_x))
    send_coords(2)
    spread(ps, (), times(to_bead, mode_p))
    others(lambda t: remote(ps.at[t], pbuf.at[me], s_p, r_p, t, dom).start())
    pbuf[me] = ps[me]

    gather_coords(2)
    all_features(2)
    arrived(pbuf.at[some], r_p)

    def finish(done):
        for b, parts in done:
            for c, f in enumerate(parts):
                x_out[c, :, lanes(b)] = ext[2, HALO + b, c]
                p_out[c, :, lanes(b)] = pbuf[b, c] + half_step * f

    forces(2, nb, lambda i: i, finish)

    arrived(xin.at[some], s_in.at[0])
    arrived(pin.at[some], s_in.at[1])
    arrived(nin.at[0, some], s_in.at[2])
    arrived(nin.at[1, some], s_in.at[3])
    for turn in range(2):
        arrived(fin.at[turn, some], s_f.at[turn])
        arrived(xs.at[turn, some], s_x.at[turn])

        @pl.when(jnp.logical_or(jnp.logical_and(lower, me < HALO), jnp.logical_and(upper, me >= nb - HALO)))
        def _():
            arrived(xs.at[turn], s_xh.at[turn])

    arrived(ps.at[some], s_p)

    @pl.when(lower)
    def _():
        for copy in down():
            copy.wait_send()

    @pl.when(upper)
    def _():
        for copy in up():
            copy.wait_send()


def solution(mesh):
    nb, ns = mesh.shape["bead"], mesh.shape["space"]

    def body(positions, momenta, atom_types, neighbours, thermal_noise):
        matrix = mode_matrix(nb)
        vmem = pl.BlockSpec(memory_space=pltpu.VMEM)
        piece = (3, 1, LANES)
        dma = pltpu.SemaphoreType.DMA
        return pl.pallas_call(
            functools.partial(kernel, nb, ns),
            out_shape=(
                jax.ShapeDtypeStruct(positions.shape, F32),
                jax.ShapeDtypeStruct(momenta.shape, F32),
            ),
            in_specs=[pl.BlockSpec(memory_space=pltpu.SMEM)]
            + [pl.BlockSpec(memory_space=pltpu.HBM)] * 8,
            out_specs=(vmem, vmem),
            scratch_shapes=[
                pltpu.VMEM(positions.shape, F32),
                pltpu.VMEM((nb, LANES), jnp.int32),
                pltpu.VMEM((2 * HALO + 1, ROWS, LANES), BF16),
                pltpu.VMEM((nb, nb), F32),
                pltpu.VMEM((nb, nb), F32),
                pltpu.VMEM((5, nb, LANES), F32),
                pltpu.VMEM((nb, *piece), F32),
                pltpu.VMEM((nb, *piece), F32),
                pltpu.VMEM((2, nb, *piece), F32),
                pltpu.VMEM((3, nb + 2 * HALO, *piece), F32),
                pltpu.VMEM((nb + 2 * HALO, 1, LANES), F32),
                pltpu.VMEM((2, nb, *piece), F32),
                pltpu.VMEM((2, nb, *piece), F32),
                pltpu.VMEM((2, nb, *piece), F32),
                pltpu.VMEM((nb, *piece), F32),
                pltpu.VMEM((nb, *piece), F32),
                pltpu.VMEM((6, nb, LANES), F32),
                pltpu.VMEM((nb + 2 * HALO, LANES, ROWS), BF16),
                pltpu.VMEM((nb + 2 * HALO, 16, LANES), BF16),
                pltpu.VMEM((nb, ROWS, LANES), BF16),
                dma((4,)),
                dma((4,)),
                dma((4,)),
                dma((4,)),
                dma((2,)),
                dma((2,)),
                dma((2,)),
                dma((2,)),
                dma((2,)),
                dma((2, 2)),
                dma,
                dma,
                dma((9,)),
                pltpu.VMEM((NBR, LANES, LANES), F32),
                pltpu.VMEM((NBR, LANES, LANES), F32),
            ],
            compiler_params=pltpu.CompilerParams(
                collective_id=0, has_side_effects=True
            ),
            name="path_integral_steps",
        )(
            neighbours.T,
            positions,
            momenta,
            thermal_noise,
            atom_types.reshape(nb, LANES),
            jnp.asarray(shift_table(), BF16),
            jnp.asarray(matrix.T.copy()),
            jnp.asarray(matrix),
            jnp.asarray(mode_tables(nb)),
        )

    spec = P(None, "bead", "space")
    return jax.shard_map(
        body,
        mesh=mesh,
        in_specs=(spec, spec, P("space"), P("space", None), P(None, None, "bead", "space")),
        out_specs=(spec, spec),
        check_vma=False,
    )
```

```python
import functools
import math

import jax
import jax.numpy as jnp
import numpy as np
from jax import lax
from jax.experimental import pallas as pl
from jax.experimental.pallas import tpu as pltpu
from jax.sharding import PartitionSpec as P

MESH = pl.DeviceIdType.MESH
F32 = jnp.float32
BF16 = jnp.bfloat16
LANES = 128
HALO = 4
NBR = 5
ROWS = 48
GROUP = 8
half_step = 0.025
time_step = 0.05
chain_freq = 12.0
thermal = 0.375
screening = 4.0
softening = 0.09
decay = math.log2(math.e) / screening
highest = lax.Precision.HIGHEST


def mode_matrix(n):
    j = np.arange(n)[:, None]
    k = np.arange(n)[None, :]
    phase = 2.0 * np.pi * j * k / n
    plain, paired = 1.0 / math.sqrt(n), math.sqrt(2.0 / n)
    return np.where(
        k == 0,
        plain,
        np.where(
            k < n // 2,
            paired * np.cos(phase),
            np.where(k == n // 2, plain * np.cos(phase), paired * np.sin(phase)),
        ),
    ).astype(np.float32)


def mode_tables(n):
    k = np.arange(n)
    w = 2.0 * chain_freq * np.sin(np.pi * k / n)
    angle = w * time_step
    ratio = np.where(k == 0, time_step, np.sin(angle) / np.where(k == 0, 1.0, w))
    friction = np.where(k == 0, 1.0, 2.0 * w)
    damping = np.exp(-friction * time_step)
    kick = np.sqrt(1.0 - damping * damping)
    tables = np.stack([np.cos(angle), ratio, w * np.sin(angle), damping, kick])
    return np.repeat(tables[:, :, None], LANES, axis=2).astype(np.float32)


def shift_table():
    parts = {0: (0, 0), 1: (1, 0), 2: (2, 0), 3: (2, 1), 4: (4, 0)}
    table = np.ones((2 * HALO + 1, ROWS), np.float32)
    for s in range(-HALO, HALO + 1):
        sign = -1 if s < 0 else 1
        one, two = parts[abs(s)]
        table[s + HALO, 27] = s * s
        table[s + HALO, 28:32] = -2 * s
        table[s + HALO, 32:36] = sign * one
        table[s + HALO, 36:40] = sign * two
    return np.repeat(table[:, :, None], LANES, axis=2)


def charge_of(types):
    return jnp.where(
        types == 0, 1.0, jnp.where(types == 1, -1.0, jnp.where(types == 2, 0.6, -1.4))
    ).astype(F32)


def three(v):
    high = v.astype(BF16).astype(F32)
    rest = v - high
    mid = rest.astype(BF16).astype(F32)
    return high, mid, rest - mid


def kernel(
    nb,
    ns,
    lists,
    x_hbm,
    p_hbm,
    noise_hbm,
    types_hbm,
    mult_hbm,
    to_mode_hbm,
    to_bead_hbm,
    tab_hbm,
    x_out,
    p_out,
    x_ref,
    types_ref,
    mult_ref,
    to_mode,
    to_bead,
    tab_ref,
    p_ref,
    xin,
    nin,
    ext,
    extq,
    fout,
    fin,
    xs,
    ps,
    pbuf,
    modes,
    fe,
    fb,
    fa,
    s_in,
    r_in,
    s_h,
    r_h,
    s_f,
    r_f,
    s_x,
    r_x,
    s_xh,
    r_xh,
    s_p,
    r_p,
    s_own,
    even,
    odd,
):
    me = lax.axis_index("bead")
    dom = lax.axis_index("space")
    first = dom * nb
    lower, upper = dom > 0, dom < ns - 1

    def lanes(block):
        return pl.ds(pl.multiple_of(block * LANES, LANES), LANES)

    def remote(src, dst, send, recv, bead, space):
        return pltpu.make_async_remote_copy(
            src_ref=src,
            dst_ref=dst,
            send_sem=send,
            recv_sem=recv,
            device_id=(bead, space),
            device_id_type=MESH,
        )

    def arrived(ref, sem):
        pltpu.make_async_copy(ref, ref, sem).wait()

    def others(body):
        def step(i, carry):
            body(lax.rem(me + i, nb))
            return carry

        lax.fori_loop(1, nb, step, 0)

    def far_first(i, count, centre):
        step = lax.div(i + 1, 2)
        return lax.rem(centre + count // 2 + count + jnp.where(i % 2 == 1, -step, step), count)

    def loop(begin, end, body):
        def step(i, carry):
            body(i)
            return carry

        lax.fori_loop(begin, end, step, 0)

    staged = [
        pltpu.make_async_copy(src, dst, s_own.at[i])
        for i, (src, dst) in enumerate(
            [
                (x_hbm, x_ref),
                (types_hbm, types_ref),
                (mult_hbm, mult_ref),
                (to_mode_hbm, to_mode),
                (to_bead_hbm, to_bead),
                (tab_hbm, tab_ref),
                (p_hbm, p_ref),
                (noise_hbm.at[:, :, :, lanes(me)], nin.at[me]),
            ]
        )
    ]
    for copy in staged:
        copy.start()

    barrier = pltpu.get_barrier_semaphore()

    def greet(bead, space):
        pl.semaphore_signal(barrier, inc=1, device_id=(bead, space), device_id_type=MESH)

    others(lambda t: greet(t, dom))

    @pl.when(lower)
    def _():
        loop(nb - HALO, nb, lambda t: greet(t, dom - 1))

        @pl.when(me < nb - HALO)
        def _():
            greet(me, dom - 1)

    @pl.when(upper)
    def _():
        loop(0, HALO, lambda t: greet(t, dom + 1))

        @pl.when(me >= HALO)
        def _():
            greet(me, dom + 1)

    row8 = lax.broadcasted_iota(jnp.int32, (4, LANES), 0)
    last = row8 == 3
    ones4 = jnp.ones((4, LANES), F32)
    zero4 = jnp.zeros((4, LANES), F32)
    minus4 = jnp.where(last, 0.0, -1.0)

    def centred(turn, n):
        return [ext[turn, n, c] - 1.0 for c in range(3)]

    def features(turn, blocks, own):
        for n, (left, heavy, right) in [(n, one_features(turn, n, own)) for n in blocks]:
            fe[n] = left
            fb[n] = heavy
            if own:
                fa[n - HALO] = right

    def own_features(turn):
        loop(0, nb // 8, lambda i: features(turn, [HALO + 8 * i + k for k in range(8)], True))

    def halo_features(turn):
        features(turn, [k for k in range(HALO)] + [nb + HALO + k for k in range(HALO)], False)

    def one_features(turn, n, own):
        right = None
        x, y, z = centred(turn, n)
        q = extq[n]
        norm = x * x + y * y + z * z
        v = jnp.concatenate(
            [x, y, z, norm, norm + softening, norm, norm, norm], axis=0
        )
        high, mid, low = three(v)
        h4, m4, l4 = high[0:4], mid[0:4], low[0:4]
        hx, mx, lx = high[0:1], mid[0:1], low[0:1]
        split_x = jnp.concatenate([hx, mx, lx, jnp.zeros_like(hx)], axis=0)
        left = jnp.concatenate(
            [h4, m4, l4, h4, m4, h4, ones4, split_x, minus4, minus4, zero4, zero4],
            axis=0,
        )
        heavy = jnp.concatenate([x, y, z, jnp.ones_like(x)], axis=0) * q
        qh, qm, ql = three(heavy)
        heavy = jnp.concatenate([qh, qm, ql, zero4], axis=0).astype(BF16)
        if own:
            ah = jnp.where(last, 1.0, -2.0 * h4)
            am = jnp.where(last, 0.0, -2.0 * m4)
            al = jnp.where(last, 0.0, -2.0 * l4)
            square = jnp.concatenate(
                [high[4:5], mid[4:5], low[4:5], jnp.ones_like(x)], axis=0
            )
            unit = jnp.where(last, 0.0, 1.0)
            twice = -2.0 * split_x
            right = jnp.concatenate(
                [ah, ah, ah, am, am, al, square, unit, twice, twice, zero4, zero4],
                axis=0,
            )
            right = right.astype(BF16)
        return left.T.astype(BF16), heavy, right

    def squares(b, ref):
        base = fa[b]
        for m in range(NBR):
            listed = lists[m, b]
            n = jnp.clip(listed - first + HALO, 0, nb + 2 * HALO - 1)
            s = jnp.clip(first + b - listed, -HALO, HALO)
            right = base * mult_ref[s + HALO]
            ref[m] = jnp.dot(fe[n], right, preferred_element_type=F32)

    def force(turn, b, ref):
        total = jnp.zeros((16, LANES), F32)
        moved = jnp.zeros((16, LANES), F32)
        for m in range(NBR):
            listed = lists[m, b]
            n = jnp.clip(listed - first + HALO, 0, nb + 2 * HALO - 1)
            s = jnp.clip(first + b - listed, -HALO, HALO)
            square = ref[m]
            r = lax.rsqrt(square)
            weight = jnp.exp2((square * r) * (-decay)) * ((r * r) * (r + 0.25))
            high = weight.astype(BF16)
            low = (weight - high.astype(F32)).astype(BF16)
            left = fb[n]
            part = jnp.dot(
                jnp.concatenate([left, left], axis=1),
                jnp.concatenate([high, low], axis=0),
                preferred_element_type=F32,
            )
            total = total + part
            moved = moved + s.astype(F32) * part
        sums = total[0:4] + total[4:8] + total[8:12]
        shifted = moved[3:4] + moved[7:8] + moved[11:12]
        x, y, z = centred(turn, b + HALO)
        q = extq[b + HALO]
        plain = sums[3:4]
        fx = q * (x * plain + shifted - sums[0:1])
        fy = q * (y * plain - sums[1:2])
        fz = q * (z * plain - sums[2:3])
        return fx, fy, fz

    def forces(turn, count, block_of, take):
        squares(block_of(0), even)
        group = next(g for g in (GROUP, 4, 2) if count % g == 0)

        def several(i):
            blocks = [block_of(lax.rem(group * i + k, count)) for k in range(group + 1)]
            done = []
            for k in range(group):
                here, there = (odd, even) if k % 2 else (even, odd)
                squares(blocks[k + 1], there)
                done.append((blocks[k], force(turn, blocks[k], here)))
            take(done)

        loop(0, count // group, several)

    def keep_force(turn):
        def take(done):
            for b, parts in done:
                for c in range(3):
                    if turn == 0:
                        fout[0, b, c] = p_ref[c, :, lanes(b)] + half_step * parts[c]
                    else:
                        fout[turn, b, c] = parts[c]

        return take

    def send_force(turn, b):
        @pl.when(b != me)
        def _():
            remote(fout.at[turn, b], fin.at[turn, me], s_f.at[turn], r_f.at[turn], b, dom).start()

    def send_forces(turn):
        def take(done):
            keep_force(turn)(done)
            for b, _ in done:
                send_force(turn, b)

        return take

    def gather_force(turn):
        fin[turn, me] = fout[turn, me]
        arrived(fin.at[turn, pl.ds(0, nb - 1)], r_f.at[turn])

    def load_own(b):
        ext[0, HALO + b] = x_ref[:, :, lanes(b)]
        extq[HALO + b] = charge_of(types_ref[pl.ds(b, 1), :])

    staged[0].wait()
    staged[1].wait()
    loop(0, nb, load_own)

    @pl.when(jnp.logical_not(lower))
    def _():
        for t in range(3):
            ext[t, 0:HALO] = jnp.zeros((HALO, 3, 1, LANES), F32)
        extq[0:HALO] = jnp.zeros((HALO, 1, LANES), F32)

    @pl.when(jnp.logical_not(upper))
    def _():
        for t in range(3):
            ext[t, nb + HALO : nb + 2 * HALO] = jnp.zeros((HALO, 3, 1, LANES), F32)
        extq[nb + HALO : nb + 2 * HALO] = jnp.zeros((HALO, 1, LANES), F32)

    own_features(0)
    staged[6].wait()
    staged[2].wait()
    inner = nb - 2 * HALO
    early = inner // 24 * 8 if inner >= 24 else inner // 6 * 2
    late = inner - early

    def inner_block(i):
        return HALO + far_first(i, inner, jnp.clip(me - HALO, 0, inner - 1))

    if early > 0:
        forces(0, early, inner_block, keep_force(0))

    senders = (
        nb
        - 1
        + jnp.where(lower, jnp.where(me < HALO, nb, 1), 0)
        + jnp.where(upper, jnp.where(me >= nb - HALO, nb, 1), 0)
    )
    pl.semaphore_wait(barrier, senders)

    low_edge, low_halo = pl.ds(HALO, HALO), pl.ds(0, HALO)
    high_edge, high_halo = pl.ds(nb, HALO), pl.ds(nb + HALO, HALO)

    def down():
        return [
            remote(ext.at[0, low_edge], ext.at[0, high_halo], s_h.at[0], r_h.at[0], me, dom - 1),
            remote(extq.at[low_edge], extq.at[high_halo], s_h.at[1], r_h.at[1], me, dom - 1),
        ]

    def up():
        return [
            remote(ext.at[0, high_edge], ext.at[0, low_halo], s_h.at[2], r_h.at[2], me, dom + 1),
            remote(extq.at[high_edge], extq.at[low_halo], s_h.at[3], r_h.at[3], me, dom + 1),
        ]

    @pl.when(lower)
    def _():
        for copy in down():
            copy.start()

    @pl.when(upper)
    def _():
        for copy in up():
            copy.start()

    def send_start(t):
        remote(x_hbm.at[:, :, lanes(t)], xin.at[me], s_in.at[0], r_in.at[0], t, dom).start()
        remote(noise_hbm.at[:, :, :, lanes(t)], nin.at[me], s_in.at[1], r_in.at[1], t, dom).start()

    others(send_start)
    xin[me] = x_ref[:, :, lanes(me)]
    if early > 0:
        loop(0, early, lambda i: send_force(0, inner_block(i)))
    @pl.when(upper)
    def _():
        arrived(ext.at[0, high_halo], r_h.at[0])
        arrived(extq.at[high_halo], r_h.at[1])

    @pl.when(lower)
    def _():
        arrived(ext.at[0, low_halo], r_h.at[2])
        arrived(extq.at[low_halo], r_h.at[3])

    halo_features(0)

    def edge(i):
        spot = lax.rem(me + i, 2 * HALO)
        return jnp.where(spot < HALO, spot, spot + inner)

    forces(0, 2 * HALO, edge, send_forces(0))
    if late > 0:
        forces(0, late, lambda i: inner_block(early + i), send_forces(0))


    for i in (3, 4, 5, 7):
        staged[i].wait()
    mass = (types_ref[pl.ds(me, 1), :] + 1).astype(F32)
    width = jnp.sqrt(thermal * mass)
    inverse = 1.0 / mass
    cosine, ratio, stiffness, damping, kick = [tab_ref[i] for i in range(5)]

    def component(ref, lead, c):
        return jnp.concatenate([ref[(*lead, j, c)] for j in range(nb)], axis=0)

    def times(matrix, parts):
        whole = jnp.concatenate(parts, axis=1)
        out = jnp.dot(matrix[...], whole, precision=highest, preferred_element_type=F32)
        return [out[:, LANES * i : LANES * (i + 1)] for i in range(len(parts))]

    def drift(turn, mode_x, mode_p):
        next_x, next_p = [], []
        for c in range(3):
            noise = jnp.concatenate([nin[j, turn, c] for j in range(nb)], axis=0)
            p_new = damping * mode_p[c] + kick * width * noise
            next_x.append(cosine * mode_x[c] + ratio * p_new * inverse)
            next_p.append(cosine * p_new - stiffness * mass * mode_x[c])
        return next_x, next_p

    def spread(ref, lead, parts):
        for c in range(3):
            for j in range(nb):
                ref[(*lead, j, c)] = parts[c][j : j + 1]

    side = nb // 4
    own_side = lax.div(me, side)
    low_owner = jnp.logical_and(lower, me < HALO)
    high_owner = jnp.logical_and(upper, me >= nb - HALO)

    def send_coords(turn):
        def inside(t):
            remote(
                xs.at[turn - 1, t],
                ext.at[turn, HALO + me],
                s_x.at[turn - 1],
                r_x.at[turn - 1, own_side],
                t,
                dom,
            ).start()

        def across(t, slot, which, space):
            remote(
                xs.at[turn - 1, t],
                ext.at[turn, slot],
                s_xh.at[turn - 1],
                r_xh.at[turn - 1, which],
                t,
                space,
            ).start()

            @pl.when(t != me)
            def _():
                inside(t)

        @pl.when(low_owner)
        def _():
            loop(0, nb, lambda i: across(far_first(i, nb, me), nb + HALO + me, 0, dom - 1))

        @pl.when(high_owner)
        def _():
            loop(0, nb, lambda i: across(far_first(i, nb, me), me - (nb - HALO), 1, dom + 1))

        @pl.when(jnp.logical_not(jnp.logical_or(low_owner, high_owner)))
        def _():
            loop(0, nb - 1, lambda i: inside(far_first(i, nb, me)))

        ext[turn, HALO + me] = xs[turn - 1, me]

    def gather_features(turn):
        for k in (0, 1, 3, 2):
            which = lax.rem(own_side + k, 4)
            arrived(
                ext.at[turn, pl.ds(0, side - 1 if k == 0 else side)],
                r_x.at[turn - 1, which],
            )
            features(turn, [HALO + side * which + i for i in range(side)], True)

        @pl.when(upper)
        def _():
            arrived(ext.at[turn, pl.ds(0, HALO)], r_xh.at[turn - 1, 0])

        @pl.when(lower)
        def _():
            arrived(ext.at[turn, pl.ds(0, HALO)], r_xh.at[turn - 1, 1])

        halo_features(turn)

    some = pl.ds(0, nb - 1)
    arrived(xin.at[some], r_in.at[0])
    arrived(nin.at[some], r_in.at[1])
    parts = times(to_mode, [component(xin, (), c) for c in range(3)])
    for c in range(3):
        modes[c] = parts[c]
    gather_force(0)
    kicked = times(to_mode, [component(fin, (0,), c) for c in range(3)])
    mode_x, mode_p = drift(0, [modes[c] for c in range(3)], kicked)
    spread(xs, (0,), times(to_bead, mode_x))
    send_coords(1)
    for c in range(3):
        modes[c] = mode_x[c]
        modes[3 + c] = mode_p[c]

    gather_features(1)
    forces(1, nb, lambda i: far_first(i, nb, me), send_forces(1))
    gather_force(1)
    kicks = times(to_mode, [component(fin, (1,), c) for c in range(3)])
    mode_x, mode_p = drift(
        1,
        [modes[c] for c in range(3)],
        [modes[3 + c] + 2.0 * half_step * kicks[c] for c in range(3)],
    )
    spread(xs, (1,), times(to_bead, mode_x))
    send_coords(2)
    spread(ps, (), times(to_bead, mode_p))
    others(lambda t: remote(ps.at[t], pbuf.at[me], s_p, r_p, t, dom).start())
    pbuf[me] = ps[me]

    gather_features(2)
    arrived(pbuf.at[some], r_p)

    def finish(done):
        for b, parts in done:
            for c, f in enumerate(parts):
                x_out[c, :, lanes(b)] = ext[2, HALO + b, c]
                p_out[c, :, lanes(b)] = pbuf[b, c] + half_step * f

    forces(2, nb, lambda i: i, finish)

    arrived(xin.at[some], s_in.at[0])
    arrived(nin.at[some], s_in.at[1])
    for turn in range(2):
        arrived(fin.at[turn, some], s_f.at[turn])
        arrived(xs.at[turn, some], s_x.at[turn])

        @pl.when(jnp.logical_or(low_owner, high_owner))
        def _():
            arrived(xs.at[turn], s_xh.at[turn])

    arrived(ps.at[some], s_p)

    @pl.when(lower)
    def _():
        for copy in down():
            copy.wait_send()

    @pl.when(upper)
    def _():
        for copy in up():
            copy.wait_send()


def solution(mesh):
    nb, ns = mesh.shape["bead"], mesh.shape["space"]

    def body(positions, momenta, atom_types, neighbours, thermal_noise):
        matrix = mode_matrix(nb)
        vmem = pl.BlockSpec(memory_space=pltpu.VMEM)
        piece = (3, 1, LANES)
        dma = pltpu.SemaphoreType.DMA
        return pl.pallas_call(
            functools.partial(kernel, nb, ns),
            out_shape=(
                jax.ShapeDtypeStruct(positions.shape, F32),
                jax.ShapeDtypeStruct(momenta.shape, F32),
            ),
            in_specs=[pl.BlockSpec(memory_space=pltpu.SMEM)]
            + [pl.BlockSpec(memory_space=pltpu.HBM)] * 8,
            out_specs=(vmem, vmem),
            scratch_shapes=[
                pltpu.VMEM(positions.shape, F32),
                pltpu.VMEM((nb, LANES), jnp.int32),
                pltpu.VMEM((2 * HALO + 1, ROWS, LANES), BF16),
                pltpu.VMEM((nb, nb), F32),
                pltpu.VMEM((nb, nb), F32),
                pltpu.VMEM((5, nb, LANES), F32),
                pltpu.VMEM(momenta.shape, F32),
                pltpu.VMEM((nb, *piece), F32),
                pltpu.VMEM((nb, 2, *piece), F32),
                pltpu.VMEM((3, nb + 2 * HALO, *piece), F32),
                pltpu.VMEM((nb + 2 * HALO, 1, LANES), F32),
                pltpu.VMEM((2, nb, *piece), F32),
                pltpu.VMEM((2, nb, *piece), F32),
                pltpu.VMEM((2, nb, *piece), F32),
                pltpu.VMEM((nb, *piece), F32),
                pltpu.VMEM((nb, *piece), F32),
                pltpu.VMEM((6, nb, LANES), F32),
                pltpu.VMEM((nb + 2 * HALO, LANES, ROWS), BF16),
                pltpu.VMEM((nb + 2 * HALO, 16, LANES), BF16),
                pltpu.VMEM((nb, ROWS, LANES), BF16),
                dma((2,)),
                dma((2,)),
                dma((4,)),
                dma((4,)),
                dma((2,)),
                dma((2,)),
                dma((2,)),
                dma((2, 4)),
                dma((2,)),
                dma((2, 2)),
                dma,
                dma,
                dma((8,)),
                pltpu.VMEM((NBR, LANES, LANES), F32),
                pltpu.VMEM((NBR, LANES, LANES), F32),
            ],
            compiler_params=pltpu.CompilerParams(
                collective_id=0, has_side_effects=True
            ),
            name="path_integral_steps",
        )(
            neighbours.T,
            positions,
            momenta,
            thermal_noise,
            atom_types.reshape(nb, LANES),
            jnp.asarray(shift_table(), BF16),
            jnp.asarray(matrix.T.copy()),
            jnp.asarray(matrix),
            jnp.asarray(mode_tables(nb)),
        )

    spec = P(None, "bead", "space")
    return jax.shard_map(
        body,
        mesh=mesh,
        in_specs=(spec, spec, P("space"), P("space", None), P(None, None, "bead", "space")),
        out_specs=(spec, spec),
        check_vma=False,
    )
```

```python
import functools
import math

import jax
import jax.numpy as jnp
import numpy as np
from jax import lax
from jax.experimental import pallas as pl
from jax.experimental.pallas import tpu as pltpu
from jax.sharding import PartitionSpec as P

MESH = pl.DeviceIdType.MESH
F32 = jnp.float32
BF16 = jnp.bfloat16
LANES = 128
HALO = 4
NBR = 5
ROWS = 48
GROUP = 8
half_step = 0.025
time_step = 0.05
chain_freq = 12.0
thermal = 0.375
screening = 4.0
softening = 0.09
decay = math.log2(math.e) / screening
highest = lax.Precision.HIGHEST


def mode_matrix(n):
    j = np.arange(n)[:, None]
    k = np.arange(n)[None, :]
    phase = 2.0 * np.pi * j * k / n
    plain, paired = 1.0 / math.sqrt(n), math.sqrt(2.0 / n)
    return np.where(
        k == 0,
        plain,
        np.where(
            k < n // 2,
            paired * np.cos(phase),
            np.where(k == n // 2, plain * np.cos(phase), paired * np.sin(phase)),
        ),
    ).astype(np.float32)


def mode_tables(n):
    k = np.arange(n)
    w = 2.0 * chain_freq * np.sin(np.pi * k / n)
    angle = w * time_step
    ratio = np.where(k == 0, time_step, np.sin(angle) / np.where(k == 0, 1.0, w))
    friction = np.where(k == 0, 1.0, 2.0 * w)
    damping = np.exp(-friction * time_step)
    kick = np.sqrt(1.0 - damping * damping)
    tables = np.stack([np.cos(angle), ratio, w * np.sin(angle), damping, kick])
    return np.repeat(tables[:, :, None], LANES, axis=2).astype(np.float32)


def shift_table():
    parts = {0: (0, 0), 1: (1, 0), 2: (2, 0), 3: (2, 1), 4: (4, 0)}
    table = np.ones((2 * HALO + 1, ROWS), np.float32)
    for s in range(-HALO, HALO + 1):
        sign = -1 if s < 0 else 1
        one, two = parts[abs(s)]
        table[s + HALO, 27] = s * s
        table[s + HALO, 28:32] = -2 * s
        table[s + HALO, 32:36] = sign * one
        table[s + HALO, 36:40] = sign * two
    return np.repeat(table[:, :, None], LANES, axis=2)


def charge_of(types):
    return jnp.where(
        types == 0, 1.0, jnp.where(types == 1, -1.0, jnp.where(types == 2, 0.6, -1.4))
    ).astype(F32)


def three(v):
    high = v.astype(BF16).astype(F32)
    rest = v - high
    mid = rest.astype(BF16).astype(F32)
    return high, mid, rest - mid


def kernel(
    nb,
    ns,
    lists,
    x_hbm,
    p_hbm,
    noise_hbm,
    types_hbm,
    mult_hbm,
    to_mode_hbm,
    to_bead_hbm,
    tab_hbm,
    both_out,
    x_ref,
    types_ref,
    mult_ref,
    to_mode,
    to_bead,
    tab_ref,
    p_ref,
    xin,
    nin,
    ext,
    extq,
    fout,
    fin,
    xs,
    ps,
    pbuf,
    modes,
    fe,
    fb,
    fa,
    s_in,
    r_in,
    s_h,
    r_h,
    s_f,
    r_f,
    s_x,
    r_x,
    s_xh,
    r_xh,
    s_p,
    r_p,
    s_own,
    even,
    odd,
):
    me = lax.axis_index("bead")
    dom = lax.axis_index("space")
    first = dom * nb
    lower, upper = dom > 0, dom < ns - 1

    def lanes(block):
        return pl.ds(pl.multiple_of(block * LANES, LANES), LANES)

    def remote(src, dst, send, recv, bead, space):
        return pltpu.make_async_remote_copy(
            src_ref=src,
            dst_ref=dst,
            send_sem=send,
            recv_sem=recv,
            device_id=(bead, space),
            device_id_type=MESH,
        )

    def arrived(ref, sem):
        pltpu.make_async_copy(ref, ref, sem).wait()

    def others(body):
        def step(i, carry):
            body(lax.rem(me + i, nb))
            return carry

        lax.fori_loop(1, nb, step, 0)

    def far_first(i, count, centre):
        step = lax.div(i + 1, 2)
        return lax.rem(centre + count // 2 + count + jnp.where(i % 2 == 1, -step, step), count)

    def loop(begin, end, body):
        def step(i, carry):
            body(i)
            return carry

        lax.fori_loop(begin, end, step, 0)

    staged = [
        pltpu.make_async_copy(src, dst, s_own.at[i])
        for i, (src, dst) in enumerate(
            [
                (x_hbm, x_ref),
                (types_hbm, types_ref),
                (mult_hbm, mult_ref),
                (to_mode_hbm, to_mode),
                (to_bead_hbm, to_bead),
                (tab_hbm, tab_ref),
                (p_hbm, p_ref),
                (noise_hbm.at[:, :, :, lanes(me)], nin.at[me]),
            ]
        )
    ]
    for copy in staged:
        copy.start()

    barrier = pltpu.get_barrier_semaphore()

    def greet(bead, space):
        pl.semaphore_signal(barrier, inc=1, device_id=(bead, space), device_id_type=MESH)

    others(lambda t: greet(t, dom))

    @pl.when(lower)
    def _():
        loop(nb - HALO, nb, lambda t: greet(t, dom - 1))

        @pl.when(me < nb - HALO)
        def _():
            greet(me, dom - 1)

    @pl.when(upper)
    def _():
        loop(0, HALO, lambda t: greet(t, dom + 1))

        @pl.when(me >= HALO)
        def _():
            greet(me, dom + 1)

    row8 = lax.broadcasted_iota(jnp.int32, (4, LANES), 0)
    last = row8 == 3
    ones4 = jnp.ones((4, LANES), F32)
    zero4 = jnp.zeros((4, LANES), F32)
    minus4 = jnp.where(last, 0.0, -1.0)

    def centred(turn, n):
        return [ext[turn, n, c] - 1.0 for c in range(3)]

    def features(turn, blocks, own):
        for n, (left, heavy, right) in [(n, one_features(turn, n, own)) for n in blocks]:
            fe[n] = left
            fb[n] = heavy
            if own:
                fa[n - HALO] = right

    def own_features(turn):
        loop(0, nb // 8, lambda i: features(turn, [HALO + 8 * i + k for k in range(8)], True))

    def halo_features(turn):
        features(turn, [k for k in range(HALO)] + [nb + HALO + k for k in range(HALO)], False)

    def one_features(turn, n, own):
        right = None
        x, y, z = centred(turn, n)
        q = extq[n]
        norm = x * x + y * y + z * z
        v = jnp.concatenate(
            [x, y, z, norm, norm + softening, norm, norm, norm], axis=0
        )
        high, mid, low = three(v)
        h4, m4, l4 = high[0:4], mid[0:4], low[0:4]
        hx, mx, lx = high[0:1], mid[0:1], low[0:1]
        split_x = jnp.concatenate([hx, mx, lx, jnp.zeros_like(hx)], axis=0)
        left = jnp.concatenate(
            [h4, m4, l4, h4, m4, h4, ones4, split_x, minus4, minus4, zero4, zero4],
            axis=0,
        )
        heavy = jnp.concatenate([x, y, z, jnp.ones_like(x)], axis=0) * q
        qh, qm, ql = three(heavy)
        heavy = jnp.concatenate([qh, qm, ql, zero4], axis=0).astype(BF16)
        if own:
            ah = jnp.where(last, 1.0, -2.0 * h4)
            am = jnp.where(last, 0.0, -2.0 * m4)
            al = jnp.where(last, 0.0, -2.0 * l4)
            square = jnp.concatenate(
                [high[4:5], mid[4:5], low[4:5], jnp.ones_like(x)], axis=0
            )
            unit = jnp.where(last, 0.0, 1.0)
            twice = -2.0 * split_x
            right = jnp.concatenate(
                [ah, ah, ah, am, am, al, square, unit, twice, twice, zero4, zero4],
                axis=0,
            )
            right = right.astype(BF16)
        return left.T.astype(BF16), heavy, right

    def squares(b, ref):
        base = fa[b]
        for m in range(NBR):
            listed = lists[m, b]
            n = jnp.clip(listed - first + HALO, 0, nb + 2 * HALO - 1)
            s = jnp.clip(first + b - listed, -HALO, HALO)
            right = base * mult_ref[s + HALO]
            ref[m] = jnp.dot(fe[n], right, preferred_element_type=F32)

    def force(turn, b, ref):
        total = jnp.zeros((16, LANES), F32)
        moved = jnp.zeros((16, LANES), F32)
        for m in range(NBR):
            listed = lists[m, b]
            n = jnp.clip(listed - first + HALO, 0, nb + 2 * HALO - 1)
            s = jnp.clip(first + b - listed, -HALO, HALO)
            square = ref[m]
            r = lax.rsqrt(square)
            weight = jnp.exp2((square * r) * (-decay)) * ((r * r) * (r + 0.25))
            high = weight.astype(BF16)
            left = fb[n]
            if turn > 0:
                low = (weight - high.astype(F32)).astype(BF16)
                left = jnp.concatenate([left, left], axis=1)
                high = jnp.concatenate([high, low], axis=0)
            part = jnp.dot(left, high, preferred_element_type=F32)
            total = total + part
            moved = moved + s.astype(F32) * part
        sums = total[0:4] + total[4:8] + total[8:12]
        shifted = moved[3:4] + moved[7:8] + moved[11:12]
        x, y, z = centred(turn, b + HALO)
        q = extq[b + HALO]
        plain = sums[3:4]
        fx = q * (x * plain + shifted - sums[0:1])
        fy = q * (y * plain - sums[1:2])
        fz = q * (z * plain - sums[2:3])
        return fx, fy, fz

    def forces(turn, count, block_of, take):
        squares(block_of(0), even)
        group = next(g for g in (GROUP, 4, 2) if count % g == 0)

        def several(i):
            blocks = [block_of(lax.rem(group * i + k, count)) for k in range(group + 1)]
            done = []
            for k in range(group):
                here, there = (odd, even) if k % 2 else (even, odd)
                squares(blocks[k + 1], there)
                done.append((blocks[k], force(turn, blocks[k], here)))
            take(done)

        loop(0, count // group, several)

    def keep_force(turn):
        def take(done):
            for b, parts in done:
                for c in range(3):
                    if turn == 0:
                        fout[0, b, c] = p_ref[c, :, lanes(b)] + half_step * parts[c]
                    else:
                        fout[turn, b, c] = parts[c]

        return take

    def send_force(turn, b):
        @pl.when(b != me)
        def _():
            remote(fout.at[turn, b], fin.at[turn, me], s_f.at[turn], r_f.at[turn], b, dom).start()

    def send_forces(turn):
        def take(done):
            keep_force(turn)(done)
            for b, _ in done:
                send_force(turn, b)

        return take

    def gather_force(turn):
        fin[turn, me] = fout[turn, me]
        arrived(fin.at[turn, pl.ds(0, nb - 1)], r_f.at[turn])

    def load_own(b):
        ext[0, HALO + b] = x_ref[:, :, lanes(b)]
        extq[HALO + b] = charge_of(types_ref[pl.ds(b, 1), :])

    staged[0].wait()
    staged[1].wait()
    loop(0, nb, load_own)

    @pl.when(jnp.logical_not(lower))
    def _():
        for t in range(3):
            ext[t, 0:HALO] = jnp.zeros((HALO, 3, 1, LANES), F32)
        extq[0:HALO] = jnp.zeros((HALO, 1, LANES), F32)

    @pl.when(jnp.logical_not(upper))
    def _():
        for t in range(3):
            ext[t, nb + HALO : nb + 2 * HALO] = jnp.zeros((HALO, 3, 1, LANES), F32)
        extq[nb + HALO : nb + 2 * HALO] = jnp.zeros((HALO, 1, LANES), F32)

    own_features(0)
    staged[6].wait()
    staged[2].wait()
    inner = nb - 2 * HALO
    early = inner // 24 * 8 if inner >= 24 else inner // 6 * 2
    late = inner - early

    def inner_block(i):
        return HALO + far_first(i, inner, jnp.clip(me - HALO, 0, inner - 1))

    if early > 0:
        forces(0, early, inner_block, keep_force(0))

    senders = (
        nb
        - 1
        + jnp.where(lower, jnp.where(me < HALO, nb, 1), 0)
        + jnp.where(upper, jnp.where(me >= nb - HALO, nb, 1), 0)
    )
    pl.semaphore_wait(barrier, senders)

    low_edge, low_halo = pl.ds(HALO, HALO), pl.ds(0, HALO)
    high_edge, high_halo = pl.ds(nb, HALO), pl.ds(nb + HALO, HALO)

    def down():
        return [
            remote(ext.at[0, low_edge], ext.at[0, high_halo], s_h.at[0], r_h.at[0], me, dom - 1),
            remote(extq.at[low_edge], extq.at[high_halo], s_h.at[1], r_h.at[1], me, dom - 1),
        ]

    def up():
        return [
            remote(ext.at[0, high_edge], ext.at[0, low_halo], s_h.at[2], r_h.at[2], me, dom + 1),
            remote(extq.at[high_edge], extq.at[low_halo], s_h.at[3], r_h.at[3], me, dom + 1),
        ]

    @pl.when(lower)
    def _():
        for copy in down():
            copy.start()

    @pl.when(upper)
    def _():
        for copy in up():
            copy.start()

    def send_start(t):
        remote(x_hbm.at[:, :, lanes(t)], xin.at[me], s_in.at[0], r_in.at[0], t, dom).start()
        remote(noise_hbm.at[:, :, :, lanes(t)], nin.at[me], s_in.at[1], r_in.at[1], t, dom).start()

    others(send_start)
    xin[me] = x_ref[:, :, lanes(me)]
    if early > 0:
        loop(0, early, lambda i: send_force(0, inner_block(i)))
    @pl.when(upper)
    def _():
        arrived(ext.at[0, high_halo], r_h.at[0])
        arrived(extq.at[high_halo], r_h.at[1])

    @pl.when(lower)
    def _():
        arrived(ext.at[0, low_halo], r_h.at[2])
        arrived(extq.at[low_halo], r_h.at[3])

    halo_features(0)

    def edge(i):
        spot = lax.rem(me + i, 2 * HALO)
        return jnp.where(spot < HALO, spot, spot + inner)

    forces(0, 2 * HALO, edge, send_forces(0))
    if late > 0:
        forces(0, late, lambda i: inner_block(early + i), send_forces(0))


    for i in (3, 4, 5, 7):
        staged[i].wait()
    mass = (types_ref[pl.ds(me, 1), :] + 1).astype(F32)
    width = jnp.sqrt(thermal * mass)
    inverse = 1.0 / mass
    cosine, ratio, stiffness, damping, kick = [tab_ref[i] for i in range(5)]

    def component(ref, lead, c):
        return jnp.concatenate([ref[(*lead, j, c)] for j in range(nb)], axis=0)

    def times(matrix, parts):
        whole = jnp.concatenate(parts, axis=1)
        out = jnp.dot(matrix[...], whole, precision=highest, preferred_element_type=F32)
        return [out[:, LANES * i : LANES * (i + 1)] for i in range(len(parts))]

    def drift(turn, mode_x, mode_p):
        next_x, next_p = [], []
        for c in range(3):
            noise = jnp.concatenate([nin[j, turn, c] for j in range(nb)], axis=0)
            p_new = damping * mode_p[c] + kick * width * noise
            next_x.append(cosine * mode_x[c] + ratio * p_new * inverse)
            next_p.append(cosine * p_new - stiffness * mass * mode_x[c])
        return next_x, next_p

    def spread(ref, lead, parts):
        for c in range(3):
            for j in range(nb):
                ref[(*lead, j, c)] = parts[c][j : j + 1]

    side = nb // 4
    own_side = lax.div(me, side)
    low_owner = jnp.logical_and(lower, me < HALO)
    high_owner = jnp.logical_and(upper, me >= nb - HALO)

    def send_coords(turn):
        def inside(t):
            remote(
                xs.at[turn - 1, t],
                ext.at[turn, HALO + me],
                s_x.at[turn - 1],
                r_x.at[turn - 1, own_side],
                t,
                dom,
            ).start()

        def across(t, slot, which, space):
            remote(
                xs.at[turn - 1, t],
                ext.at[turn, slot],
                s_xh.at[turn - 1],
                r_xh.at[turn - 1, which],
                t,
                space,
            ).start()

            @pl.when(t != me)
            def _():
                inside(t)

        @pl.when(low_owner)
        def _():
            loop(0, nb, lambda i: across(far_first(i, nb, me), nb + HALO + me, 0, dom - 1))

        @pl.when(high_owner)
        def _():
            loop(0, nb, lambda i: across(far_first(i, nb, me), me - (nb - HALO), 1, dom + 1))

        @pl.when(jnp.logical_not(jnp.logical_or(low_owner, high_owner)))
        def _():
            loop(0, nb - 1, lambda i: inside(far_first(i, nb, me)))

        ext[turn, HALO + me] = xs[turn - 1, me]

    def gather_features(turn):
        for k in (0, 1, 3, 2):
            which = lax.rem(own_side + k, 4)
            arrived(
                ext.at[turn, pl.ds(0, side - 1 if k == 0 else side)],
                r_x.at[turn - 1, which],
            )
            features(turn, [HALO + side * which + i for i in range(side)], True)

        @pl.when(upper)
        def _():
            arrived(ext.at[turn, pl.ds(0, HALO)], r_xh.at[turn - 1, 0])

        @pl.when(lower)
        def _():
            arrived(ext.at[turn, pl.ds(0, HALO)], r_xh.at[turn - 1, 1])

        halo_features(turn)

    some = pl.ds(0, nb - 1)
    arrived(xin.at[some], r_in.at[0])
    arrived(nin.at[some], r_in.at[1])
    parts = times(to_mode, [component(xin, (), c) for c in range(3)])
    for c in range(3):
        modes[c] = parts[c]
    gather_force(0)
    kicked = times(to_mode, [component(fin, (0,), c) for c in range(3)])
    mode_x, mode_p = drift(0, [modes[c] for c in range(3)], kicked)
    spread(xs, (0,), times(to_bead, mode_x))
    send_coords(1)
    for c in range(3):
        modes[c] = mode_x[c]
        modes[3 + c] = mode_p[c]

    gather_features(1)
    forces(1, nb, lambda i: far_first(i, nb, me), send_forces(1))
    gather_force(1)
    kicks = times(to_mode, [component(fin, (1,), c) for c in range(3)])
    mode_x, mode_p = drift(
        1,
        [modes[c] for c in range(3)],
        [modes[3 + c] + 2.0 * half_step * kicks[c] for c in range(3)],
    )
    spread(xs, (1,), times(to_bead, mode_x))
    send_coords(2)
    spread(ps, (), times(to_bead, mode_p))
    others(lambda t: remote(ps.at[t], pbuf.at[me], s_p, r_p, t, dom).start())
    pbuf[me] = ps[me]

    gather_features(2)
    arrived(pbuf.at[some], r_p)

    def finish(done):
        for b, parts in done:
            for c, f in enumerate(parts):
                both_out[0, c, :, lanes(b)] = ext[2, HALO + b, c]
                both_out[1, c, :, lanes(b)] = pbuf[b, c] + half_step * f

    forces(2, nb, lambda i: i, finish)

    arrived(xin.at[some], s_in.at[0])
    arrived(nin.at[some], s_in.at[1])
    for turn in range(2):
        arrived(fin.at[turn, some], s_f.at[turn])
        arrived(xs.at[turn, some], s_x.at[turn])

        @pl.when(jnp.logical_or(low_owner, high_owner))
        def _():
            arrived(xs.at[turn], s_xh.at[turn])

    arrived(ps.at[some], s_p)

    @pl.when(lower)
    def _():
        for copy in down():
            copy.wait_send()

    @pl.when(upper)
    def _():
        for copy in up():
            copy.wait_send()


def solution(mesh):
    nb, ns = mesh.shape["bead"], mesh.shape["space"]

    def body(positions, momenta, atom_types, neighbours, thermal_noise):
        matrix = mode_matrix(nb)
        vmem = pl.BlockSpec(memory_space=pltpu.VMEM)
        piece = (3, 1, LANES)
        dma = pltpu.SemaphoreType.DMA
        both = pl.pallas_call(
            functools.partial(kernel, nb, ns),
            out_shape=jax.ShapeDtypeStruct((2, *positions.shape), F32),
            in_specs=[pl.BlockSpec(memory_space=pltpu.SMEM)]
            + [pl.BlockSpec(memory_space=pltpu.HBM)] * 8,
            out_specs=vmem,
            scratch_shapes=[
                pltpu.VMEM(positions.shape, F32),
                pltpu.VMEM((nb, LANES), jnp.int32),
                pltpu.VMEM((2 * HALO + 1, ROWS, LANES), BF16),
                pltpu.VMEM((nb, nb), F32),
                pltpu.VMEM((nb, nb), F32),
                pltpu.VMEM((5, nb, LANES), F32),
                pltpu.VMEM(momenta.shape, F32),
                pltpu.VMEM((nb, *piece), F32),
                pltpu.VMEM((nb, 2, *piece), F32),
                pltpu.VMEM((3, nb + 2 * HALO, *piece), F32),
                pltpu.VMEM((nb + 2 * HALO, 1, LANES), F32),
                pltpu.VMEM((2, nb, *piece), F32),
                pltpu.VMEM((2, nb, *piece), F32),
                pltpu.VMEM((2, nb, *piece), F32),
                pltpu.VMEM((nb, *piece), F32),
                pltpu.VMEM((nb, *piece), F32),
                pltpu.VMEM((6, nb, LANES), F32),
                pltpu.VMEM((nb + 2 * HALO, LANES, ROWS), BF16),
                pltpu.VMEM((nb + 2 * HALO, 16, LANES), BF16),
                pltpu.VMEM((nb, ROWS, LANES), BF16),
                dma((2,)),
                dma((2,)),
                dma((4,)),
                dma((4,)),
                dma((2,)),
                dma((2,)),
                dma((2,)),
                dma((2, 4)),
                dma((2,)),
                dma((2, 2)),
                dma,
                dma,
                dma((8,)),
                pltpu.VMEM((NBR, LANES, LANES), F32),
                pltpu.VMEM((NBR, LANES, LANES), F32),
            ],
            compiler_params=pltpu.CompilerParams(
                collective_id=0, has_side_effects=True
            ),
            name="path_integral_steps",
        )(
            neighbours.T,
            positions,
            momenta,
            thermal_noise,
            atom_types.reshape(nb, LANES),
            jnp.asarray(shift_table(), BF16),
            jnp.asarray(matrix.T.copy()),
            jnp.asarray(matrix),
            jnp.asarray(mode_tables(nb)),
        )
        return both[0], both[1]

    spec = P(None, "bead", "space")
    return jax.shard_map(
        body,
        mesh=mesh,
        in_specs=(spec, spec, P("space"), P("space", None), P(None, None, "bead", "space")),
        out_specs=(spec, spec),
        check_vma=False,
    )
```
